32 devices in a mesh: pipe: 4 (over y, x), expert: 8 (over z, core).
Axes of the slice: x: 2, y: 2, z: 4, core: 2. Of those that a mesh axis runs over, the one named last changes fastest.
Arguments:
- tokens: bfloat16 [1024, 7168], P('expert', 'pipe'), may hold values from -6 to 6
- route: int32 [1024, 1], P('expert'), may hold values from 0 to 7; in each aligned block of 128 rows (0 to 127, 128 to 255, ...) at most 24 rows name the same one
- route_weight: float32 [1024], P('expert'), may hold values from 0.2 to 1.5
- gate_up: bfloat16 [8, 2, 1024, 7168], P('expert', None, 'pipe'), may hold values from -0.0625 to 0.0625
- down: bfloat16 [8, 1024, 7168], P('expert', 'pipe'), may hold values from -0.1875 to 0.1875
Outputs:
- mixed: bfloat16 [1024, 7168], P('expert', 'pipe')
The draws below stay inside these ranges and needn't reach their ends.
Inputs may be any that keep to these rules, and one draw needn't show every extreme that they name: `route`: among the 128 rows of one index of the expert axis no expert is named more than 24 times, a bound that some block reaches.
All inputs are finite; a program needn't handle non-finite values.
Results may differ from the reference program's by a relative error of at most 0.0058.
Values may be sent and summed in bfloat16 or wider, within the bound.
No kernel may reach another device: no remote copies, remote signals or barrier semaphores. Data moves between devices by JAX's collectives and lax.ppermute only.
A program may use at most 64 MiB of HBM per device.

```python
import math
import jax
import jax.numpy as jnp
import numpy as np
from jax import lax

D = 7168
FF = 1024
TOK_DEV = 128
EXPERTS = 8
CAP = 24
TOKENS = 1024
N_EXPERT = 8


def steps_of(own_key, extent, shards, smallest, high):
    factor_of = 1.0
    for axis_at, blocks in shards:
        draws = jax.random.uniform(jax.random.fold_in(jax.random.fold_in(own_key, 6), axis_at), (blocks,), jnp.float32, smallest / len(shards), high / len(shards))
        factor_of = factor_of * jnp.repeat(jnp.exp(draws), extent[axis_at] // blocks).reshape((-1,) + (1,) * (len(extent) - 1 - axis_at))
    return factor_of


def assign_block(rng, own, number, rows, count, top, limit, slope):
    ranking = jax.random.permutation(rng, count)
    packed, usual = portions_of(count, rows * top, limit, slope, True), portions_of(count, rows * top, limit, slope, False)
    places = jnp.arange(count)

    def named(lengths, rotation):
        used = int((lengths > 0).sum())
        fixed = max(1, used // 4)
        passed = fixed + (places - fixed + rotation * (used - fixed)) % max(1, count - fixed)
        return jnp.zeros((count,), jnp.int32).at[ranking[jnp.where(places < fixed, places, passed)]].set(jnp.asarray(lengths, jnp.int32))

    lengths = jnp.where(number % 4 == 0, named(packed, number // 4), named(usual, number - number // 4 - 1))
    mixed = jax.random.permutation(jax.random.fold_in(own, 3), count)
    giver, sink = mixed[0:count // 2 * 2:2], mixed[1:count // 2 * 2:2]
    room = jnp.minimum(lengths[giver] - 1, limit - lengths[sink]) // 2
    room = jnp.where((giver == ranking[0]) | (sink == ranking[0]) | (lengths[sink] == 0), 0, jnp.maximum(room, 0))
    passed = jax.random.randint(jax.random.fold_in(own, 4), (count // 2,), 0, 1 << 20) % (room + 1)
    lengths = lengths.at[giver].add(-passed).at[sink].add(passed)
    labels = jnp.searchsorted(jnp.cumsum(lengths), jnp.arange(rows * top), side="right").astype(jnp.int32)
    table = labels.reshape(top, rows).T
    table = table[jax.random.permutation(jax.random.fold_in(own, 1), rows)]
    rotation = jax.random.randint(jax.random.fold_in(own, 2), (rows, 1), 0, top)
    return jnp.take_along_axis(table, (jnp.arange(top)[None, :] + rotation) % top, axis=1)


def portions_of(count, total, reach, skew, full):
    loads = [(1 << 20) // math.isqrt(rank ** skew) + 1 for rank in range(1, count + 1)]
    largest = reach if full else min(reach, max(-(-total // count), total * loads[0] // sum(loads)))
    least = 1 if total - largest >= count - 1 else 0
    given, spare = [largest] + [least] * (count - 1), total - largest - least * (count - 1)
    while spare > 0:
        free = [i for i in range(1, count) if given[i] < largest] or [i for i in range(1, count) if given[i] < reach]
        whole, remaining = sum([loads[i] for i in free]), spare
        for i in free:
            more = min(reach - given[i], max(1, remaining * loads[i] // whole), spare)
            given[i] = given[i] + more
            spare = spare - more
    return np.array(given)


def gaussian(rng, dims, deviation, reach, cuts=(), kind=jnp.bfloat16):
    array = deviation * jax.random.normal(rng, dims, jnp.float32)
    if cuts:
        array = array * steps_of(rng, dims, cuts, -0.22, 0.18)
    return jnp.clip(array, -reach, reach).astype(kind)


def setup_inputs(seed: int = 0) -> dict:
    keys = jax.random.split(jax.random.key(seed), 6)
    tokens = gaussian(keys[0], (TOKENS, D), 1.0, 6.0, ((0, 8), (1, 4)))
    route_keys = jax.random.split(jax.random.fold_in(keys[1], 1), TOKENS // TOK_DEV)
    route_turns = jax.random.permutation(jax.random.fold_in(keys[1], 3), TOKENS // TOK_DEV)
    route = jax.vmap(lambda own, number: assign_block(jax.random.fold_in(keys[1], 2), own, number, TOK_DEV, EXPERTS, 1, CAP, 2))(route_keys, route_turns).reshape((TOKENS, 1))
    route_weight = jnp.clip(0.2 + 1.3 * jax.random.uniform(keys[2], (TOKENS,), jnp.float32) ** steps_of(keys[2], (TOKENS,), ((0, 8),), -0.2, 0.2), 0.2, 1.5)
    gate_up = gaussian(keys[3], (EXPERTS, 2, FF, D), D ** -0.5, 0.0625, ((0, 8), (2, 4)))
    down = gaussian(keys[4], (EXPERTS, FF, D), FF ** -0.5, 0.1875, ((0, 8), (1, 4)))
    return {"tokens": tokens, "route": route, "route_weight": route_weight, "gate_up": gate_up, "down": down}


def reference(tokens, route, route_weight, gate_up, down):
    slots = CAP * N_EXPERT
    experts_ids = route[:, 0]
    total = TOK_DEV * N_EXPERT

    def per_expert(acc, inputs):
        weights_in, weights_out, which = inputs
        found = jnp.nonzero(experts_ids == which, size=slots, fill_value=0)[0].astype(jnp.int32)
        count = jnp.sum((experts_ids == which).astype(jnp.int32))
        valid = (jnp.arange(slots, dtype=jnp.int32) < count).astype(jnp.float32)
        rows = tokens[found]
        gate = jnp.dot(rows, weights_in[0].T, preferred_element_type=jnp.float32)
        upper = jnp.dot(rows, weights_in[1].T, preferred_element_type=jnp.float32)
        hidden = (jax.nn.silu(gate) * upper).astype(jnp.bfloat16)
        result = jnp.dot(hidden, weights_out, preferred_element_type=jnp.float32).astype(jnp.bfloat16)
        scaled = route_weight[found][:, None] * result.astype(jnp.float32) * valid[:, None]
        return acc.at[found].add(scaled), None

    start = jnp.zeros((total, D), jnp.float32)
    final, _ = lax.scan(per_expert, start, (gate_up, down, jnp.arange(N_EXPERT, dtype=jnp.int32)))
    return final.astype(jnp.bfloat16)
```

```python
import functools

import jax
import jax.numpy as jnp
from jax import lax
from jax.experimental import pallas as pl
from jax.experimental.pallas import tpu as pltpu
from jax.sharding import PartitionSpec as P

SUBS = 4


def serial_shards(tokens, route, route_weight, gate_up, down):
    n_expert = lax.axis_size("expert")
    tok_rows = tokens.shape[0]
    width_part = tokens.shape[1]
    capacity = max(2, 3 * tok_rows // (2 * n_expert))
    slot_total = n_expert * capacity
    chosen = route[:, 0]
    onehot = (chosen[:, None] == jnp.arange(n_expert, dtype=jnp.int32)[None, :]).astype(jnp.int32)
    position = jnp.sum(jnp.cumsum(onehot, axis=0) * onehot, axis=1) - 1
    slot_of = chosen * capacity + position
    placer = (slot_of[None, :] == jnp.arange(slot_total, dtype=jnp.int32)[:, None]).astype(
        jnp.bfloat16
    )
    packed = jnp.dot(placer, tokens, preferred_element_type=jnp.float32).astype(jnp.bfloat16)
    packed = packed.reshape(n_expert, capacity, width_part)
    local_in = gate_up[0]
    local_out = down[0]
    received = lax.all_to_all(packed, "expert", split_axis=0, concat_axis=0, tiled=True)
    sources, items, cols = received.shape
    flat_rows = received.reshape(sources * items, cols)
    both = jnp.einsum(
        "rd,sfd->rsf",
        lax.all_gather(flat_rows, "pipe", axis=1, tiled=True),
        local_in,
        preferred_element_type=jnp.float32,
    )
    hidden = (jax.nn.silu(both[:, 0]) * both[:, 1]).astype(jnp.bfloat16)
    partial_value = jnp.dot(hidden, local_out, preferred_element_type=jnp.float32)
    result = lax.psum_scatter(partial_value, "pipe", scatter_dimension=1, tiled=True).astype(
        jnp.bfloat16
    )
    result = result.reshape(sources, items, cols)
    returned = lax.all_to_all(result, "expert", split_axis=0, concat_axis=0, tiled=True)
    gathered = jnp.dot(
        placer.T, returned.reshape(slot_total, width_part), preferred_element_type=jnp.float32
    )
    return (route_weight[:, None] * gathered).astype(jnp.bfloat16)


def flip(x, axis, mask):
    return lax.ppermute(x, axis, [(i, i ^ mask) for i in range(lax.axis_size(axis))])


def expert_kernel(plan, n_pipe, rows, *refs):
    n_in = 2 + sum(len({a for a, _, _ in s[2]}) for s in plan)
    n_out = 2 * len(plan)
    gate_up, down = refs[:2]
    operands = refs[2:n_in]
    outs = refs[n_in : n_in + n_out]
    x, w_in, w_out, total, x_sem, in_sem, out_sem = refs[n_in + n_out :]
    me = lax.axis_index("pipe")
    width = x.shape[2]
    hidden_rows = gate_up.shape[2]

    def columns(piece):
        return pl.ds(pl.multiple_of((me ^ piece) * width, 128), width)

    def x_copies(piece):
        copies = []
        for at, (first, count, parts, _, _) in enumerate(plan):
            for operand, row, ident in parts:
                if ident == piece:
                    copies.append(
                        pltpu.make_async_copy(
                            operands[operand].at[pl.ds(row, count)],
                            x.at[piece, pl.ds(first, count)],
                            x_sem.at[piece, at],
                        )
                    )
        return copies

    def in_copies(piece):
        return [
            pltpu.make_async_copy(
                gate_up.at[0, s, :, columns(piece)],
                w_in.at[piece, pl.ds(s * hidden_rows, hidden_rows)],
                in_sem.at[piece, s],
            )
            for s in range(2)
        ]

    def out_copy(piece):
        return pltpu.make_async_copy(
            down.at[0, :, columns(piece)], w_out.at[piece], out_sem.at[piece]
        )

    for piece in range(n_pipe):
        for copy in x_copies(piece) + in_copies(piece):
            copy.start()
    for piece in range(n_pipe):
        out_copy(piece).start()
    for piece in range(n_pipe):
        for copy in x_copies(piece) + in_copies(piece):
            copy.wait()
        product = lax.dot_general(
            x[piece], w_in[piece], (((1,), (1,)), ((), ())), preferred_element_type=jnp.float32
        )
        if piece == 0:
            total[...] = product
        else:
            total[...] += product
    gate, up = total[:, :hidden_rows], total[:, hidden_rows:]
    hidden = (gate / (1.0 + jnp.exp(-gate)) * up).astype(jnp.bfloat16)
    for piece in range(n_pipe):
        out_copy(piece).wait()
        product = jnp.dot(hidden, w_out[piece], preferred_element_type=jnp.float32)
        for at, (first, count, _, sent, kept) in enumerate(plan):
            part = product[first : first + count]
            if piece in sent:
                i = sent.index(piece)
                outs[2 * at][i * count : (i + 1) * count] = part.astype(jnp.bfloat16)
            else:
                i = kept.index(piece)
                outs[2 * at + 1][i * count : (i + 1) * count] = part


def expert_layer(gate_up, down, chunks):
    n_pipe = lax.axis_size("pipe")
    width = chunks[0][0][0][0].shape[1]
    hidden_rows = gate_up.shape[2]
    plan, operands, shapes, first = [], [], [], 0
    for arrays, count, sent, kept in chunks:
        parts = []
        for array, ids in arrays:
            for i, ident in enumerate(ids):
                parts.append((len(operands), i * count, ident))
            operands.append(array)
        plan.append((first, count, parts, sent, kept))
        first += count
        shapes.append(jax.ShapeDtypeStruct((len(sent) * count, width), jnp.bfloat16))
        shapes.append(jax.ShapeDtypeStruct((len(kept) * count, width), jnp.float32))
    anywhere = pl.BlockSpec(memory_space=pl.ANY)
    weights = gate_up.size + down.size
    outs = pl.pallas_call(
        functools.partial(expert_kernel, plan, n_pipe, first),
        out_shape=shapes,
        in_specs=[anywhere] * (2 + len(operands)),
        out_specs=[pl.BlockSpec(memory_space=pltpu.VMEM)] * len(shapes),
        scratch_shapes=[
            pltpu.VMEM((n_pipe, first, width), jnp.bfloat16),
            pltpu.VMEM((n_pipe, 2 * hidden_rows, width), jnp.bfloat16),
            pltpu.VMEM((n_pipe, hidden_rows, width), jnp.bfloat16),
            pltpu.VMEM((first, 2 * hidden_rows), jnp.float32),
            pltpu.SemaphoreType.DMA((n_pipe, len(chunks))),
            pltpu.SemaphoreType.DMA((n_pipe, 2)),
            pltpu.SemaphoreType.DMA((n_pipe,)),
        ],
        cost_estimate=pl.CostEstimate(
            flops=2 * first * weights, bytes_accessed=2 * weights, transcendentals=0
        ),
        compiler_params=pltpu.CompilerParams(vmem_limit_bytes=40 << 20),
        name="expert_layer",
    )(gate_up, down, *operands)
    return [(outs[2 * i], outs[2 * i + 1]) for i in range(len(chunks))]


def gather(own, order):
    arrays, held = [(own, [0])], [0]
    for bit in order:
        block = jnp.concatenate([a for a, _ in arrays]) if len(arrays) > 1 else own
        arrays.append((flip(block, "pipe", bit), [i ^ bit for i in held]))
        held = held + [i ^ bit for i in held]
    return arrays


def pipelined_shards(tokens, route, route_weight, gate_up, down):
    n_expert, n_pipe = lax.axis_size("expert"), lax.axis_size("pipe")
    me = lax.axis_index("expert")
    tok_rows, width = tokens.shape
    capacity = max(2, 3 * tok_rows // (2 * n_expert))
    slots = n_expert * capacity
    bits = [1 << b for b in range(n_pipe.bit_length() - 1)]

    distance = route[:, 0] ^ me
    onehot = (distance[:, None] == jnp.arange(n_expert, dtype=jnp.int32)[None, :]).astype(jnp.int32)
    position = jnp.sum(jnp.cumsum(onehot, axis=0) * onehot, axis=1) - 1
    slot_of = distance * capacity + position
    placer = (slot_of[None, :] == jnp.arange(slots, dtype=jnp.int32)[:, None]).astype(jnp.bfloat16)
    packed = jnp.dot(placer, tokens, preferred_element_type=jnp.float32).astype(jnp.bfloat16)
    packed = packed.reshape(n_expert, capacity, width)

    per_sub = n_expert // SUBS
    count = per_sub * capacity
    received = [packed[0]] + [flip(packed[k], "expert", k) for k in range(1, n_expert)]
    subs = []
    for s in range(SUBS):
        own = jnp.concatenate(received[s * per_sub : (s + 1) * per_sub])
        order = bits if s % 2 == 0 else bits[::-1]
        subs.append((gather(own, order), order))

    results = []
    for g in range(0, SUBS, 2):
        chunks = []
        for arrays, order in subs[g : g + 2]:
            last = order[-1]
            kept = [i for i in range(n_pipe) if not i & last]
            chunks.append((arrays, count, [i ^ last for i in kept], kept))
        for (sent, kept_sum), (arrays, order), chunk in zip(
            expert_layer(gate_up, down, chunks), subs[g : g + 2], chunks
        ):
            ids = chunk[3]
            back = order[::-1]
            moved = flip(sent, "pipe", back[0])
            for at, bit in enumerate(back[1:]):
                summed = kept_sum + moved.astype(jnp.float32)
                blocks = {i: summed[n * count : (n + 1) * count] for n, i in enumerate(ids)}
                ids = [i for i in ids if not i & bit]
                send = jnp.concatenate([blocks[i ^ bit] for i in ids]).astype(jnp.bfloat16)
                kept_sum = jnp.concatenate([blocks[i] for i in ids])
                moved = flip(send, "pipe", bit)
            results.append((kept_sum + moved.astype(jnp.float32)).astype(jnp.bfloat16))

    returned = []
    for k in range(n_expert):
        block = results[k // per_sub][(k % per_sub) * capacity : (k % per_sub + 1) * capacity]
        returned.append(block if k == 0 else flip(block, "expert", k))
    gathered = jnp.dot(placer.T, jnp.concatenate(returned), preferred_element_type=jnp.float32)
    return (route_weight[:, None] * gathered).astype(jnp.bfloat16)


def solution(mesh):
    in_specs = (
        P("expert", "pipe"),
        P("expert", None),
        P("expert"),
        P("expert", None, "pipe", None),
        P("expert", "pipe", None),
    )
    out_specs = P("expert", "pipe")

    def shards(tokens, route, route_weight, gate_up, down):
        n_expert, n_pipe = mesh.shape["expert"], mesh.shape["pipe"]
        tok_rows, width = tokens.shape
        capacity = max(2, 3 * tok_rows // (2 * n_expert))
        powers = n_expert & (n_expert - 1) == 0 and n_pipe & (n_pipe - 1) == 0
        aligned = width % 128 == 0 and capacity % 8 == 0 and gate_up.shape[2] % 128 == 0
        if powers and aligned and n_expert % SUBS == 0 and n_pipe > 1:
            return pipelined_shards(tokens, route, route_weight, gate_up, down)
        return serial_shards(tokens, route, route_weight, gate_up, down)

    return jax.shard_map(shards, mesh=mesh, in_specs=in_specs, out_specs=out_specs, check_vma=False)
```

```python
import functools

import jax
import jax.numpy as jnp
from jax import lax
from jax.experimental import pallas as pl
from jax.experimental.pallas import tpu as pltpu
from jax.sharding import PartitionSpec as P


SUBS = 4
VMEM_LIMIT = 32 << 20
PACK_FLOPS = 1 << 25
FOLD_FLOPS = 1 << 33
FORMS = (('2', '2'), ('2', '2'), ('3', '3'), ('3', '3'))
GROUPS = ((3,), (2,), (1, 0))


def serial_shards(tokens, route, route_weight, gate_up, down):
    n_expert = lax.axis_size("expert")
    tok_rows = tokens.shape[0]
    width_part = tokens.shape[1]
    capacity = max(2, 3 * tok_rows // (2 * n_expert))
    slot_total = n_expert * capacity
    chosen = route[:, 0]
    onehot = (chosen[:, None] == jnp.arange(n_expert, dtype=jnp.int32)[None, :]).astype(jnp.int32)
    position = jnp.sum(jnp.cumsum(onehot, axis=0) * onehot, axis=1) - 1
    slot_of = chosen * capacity + position
    placer = (slot_of[None, :] == jnp.arange(slot_total, dtype=jnp.int32)[:, None]).astype(
        jnp.bfloat16
    )
    packed = jnp.dot(placer, tokens, preferred_element_type=jnp.float32).astype(jnp.bfloat16)
    packed = packed.reshape(n_expert, capacity, width_part)
    local_in = gate_up[0]
    local_out = down[0]
    received = lax.all_to_all(packed, "expert", split_axis=0, concat_axis=0, tiled=True)
    sources, items, cols = received.shape
    flat_rows = received.reshape(sources * items, cols)
    both = jnp.einsum(
        "rd,sfd->rsf",
        lax.all_gather(flat_rows, "pipe", axis=1, tiled=True),
        local_in,
        preferred_element_type=jnp.float32,
    )
    hidden = (jax.nn.silu(both[:, 0]) * both[:, 1]).astype(jnp.bfloat16)
    partial_value = jnp.dot(hidden, local_out, preferred_element_type=jnp.float32)
    result = lax.psum_scatter(partial_value, "pipe", scatter_dimension=1, tiled=True).astype(
        jnp.bfloat16
    )
    result = result.reshape(sources, items, cols)
    returned = lax.all_to_all(result, "expert", split_axis=0, concat_axis=0, tiled=True)
    gathered = jnp.dot(
        placer.T, returned.reshape(slot_total, width_part), preferred_element_type=jnp.float32
    )
    return (route_weight[:, None] * gathered).astype(jnp.bfloat16)


def flip(x, axis, mask):
    return lax.ppermute(x, axis, [(i, i ^ mask) for i in range(lax.axis_size(axis))])


def expert_kernel(plan, n_pipe, *refs):
    gate_up, down = refs[:2]
    me = lax.axis_index("pipe")
    width = down.shape[2] // n_pipe

    core = lax.axis_index("expert") & 1
    idents = [0, 1 + core, 2 - core, 3]

    def columns(piece):
        return pl.ds(pl.multiple_of((me ^ idents[piece]) * width, 128), width)

    gate = up = None
    for piece in range(n_pipe):
        rows = [refs[i][r : r + n] for _, parts, _ in plan for i, r, n in parts[piece]]
        rows = jnp.concatenate(rows) if len(rows) > 1 else rows[0]
        products = []
        for s in range(2):
            products.append(
                lax.dot_general(
                    rows,
                    gate_up[0, s, :, columns(piece)],
                    (((1,), (1,)), ((), ())),
                    preferred_element_type=jnp.float32,
                )
            )
        gate = products[0] if piece == 0 else gate + products[0]
        up = products[1] if piece == 0 else up + products[1]
    hidden = (gate / (1.0 + jnp.exp(-gate)) * up).astype(jnp.bfloat16)
    for piece in range(n_pipe):
        product = jnp.dot(hidden, down[0, :, columns(piece)], preferred_element_type=jnp.float32)
        first = 0
        for _, _, results in plan:
            for i, r, n in results[piece]:
                refs[i][r : r + n] = product[first : first + n].astype(refs[i].dtype)
                first += n


def expert_layer(weights, chunks):
    n_pipe = lax.axis_size("pipe")
    width = weights[1].shape[2] // n_pipe
    operands, shapes, plan = list(weights), [], []
    for _, parts, _, _ in chunks:
        for segments in parts:
            for array, _, _ in segments:
                if all(array is not o for o in operands):
                    operands.append(array)

    def place(array):
        return [array is o for o in operands].index(True)

    for count, parts, sent, kept in chunks:
        results = [[] for _ in range(n_pipe)]
        for blocks in [*sent, *[[(i, count)] for i in kept]]:
            at = 0
            for ident, rows in blocks:
                results[ident].append((len(operands) + len(shapes), at, rows))
                at += rows
            kind = jnp.bfloat16 if blocks in sent else jnp.float32
            shapes.append(jax.ShapeDtypeStruct((at, width), kind))
        plan.append((count, [[(place(a), r, n) for a, r, n in p] for p in parts], results))
    total = sum(p[0] for p in plan)
    size = sum(w.size for w in weights)
    in_vmem = pl.BlockSpec(memory_space=pltpu.VMEM)
    outs = pl.pallas_call(
        functools.partial(expert_kernel, plan, n_pipe),
        out_shape=shapes,
        in_specs=[in_vmem] * len(operands),
        out_specs=[in_vmem] * len(shapes),
        cost_estimate=pl.CostEstimate(
            flops=2 * total * size, bytes_accessed=2 * size, transcendentals=0
        ),
        compiler_params=pltpu.CompilerParams(vmem_limit_bytes=VMEM_LIMIT),
        name="expert_layer",
    )(*operands)
    outs = list(outs)
    return [[outs.pop(0) for _ in [*sent, *kept]] for _, _, sent, kept in chunks]


def swap(x, stage):
    n_pipe, n_expert = lax.axis_size("pipe"), lax.axis_size("expert")
    pairs = []
    for p in range(n_pipe):
        for e in range(n_expert):
            bit = 1 + (e & 1 ^ stage)
            pairs.append((p * n_expert + e, (p ^ bit) * n_expert + e))
    return lax.ppermute(x, ("pipe", "expert"), pairs)


def gather(own, form):
    count = own.shape[0]
    moved = swap(own, 0)
    if form == "3":
        straight = swap(own, 1)
        across = swap(moved, 1)
        return [[(a, 0, count)] for a in (own, moved, straight, across)]
    pair = jnp.concatenate([own, moved])
    pair = swap(pair, 1)
    return [[(own, 0, count)], [(moved, 0, count)], [(pair, 0, count)], [(pair, count, count)]]


def sent_first(form, count):
    if form == "3":
        return [[(3, count)], [(1, count)]], [2, 0]
    return [[(1, count), (3, count)]], [2, 0]


def sums(form, arrays):
    wide, narrow = jnp.float32, jnp.bfloat16
    *sent, piece, own = arrays
    count = own.shape[0]
    if form == "3":
        far = swap(sent[0], 0)
        near = swap(sent[1], 0)
        piece = (piece + far.astype(wide)).astype(narrow)
        return own, near, swap(piece, 1)
    pair = swap(sent[0], 0)
    piece = (piece + pair[count:].astype(wide)).astype(narrow)
    return own, pair[:count], swap(piece, 1)


def pack_kernel(capacity, tokens, distance, straight, crossed, slot_of):
    slots = 2 * straight.shape[0]
    count = tokens.shape[0]
    n_expert = slots // capacity
    distance = distance[...]
    experts = lax.broadcasted_iota(jnp.int32, (n_expert, count), 0)
    onehot = (experts == distance).astype(jnp.float32)
    before = lax.broadcasted_iota(jnp.int32, (count, count), 0)
    after = lax.broadcasted_iota(jnp.int32, (count, count), 1)
    upto = (before <= after).astype(jnp.float32).astype(jnp.bfloat16)
    ranks = jnp.dot(onehot.astype(jnp.bfloat16), upto, preferred_element_type=jnp.float32)
    position = jnp.sum(ranks * onehot, axis=0, keepdims=True).astype(jnp.int32) - 1
    slot = ((distance & 1) * (n_expert // 2) + (distance >> 1)) * capacity + position
    slot_of[...] = slot
    rows = lax.broadcasted_iota(jnp.int32, (slots, count), 0)
    placer = (rows == slot).astype(jnp.float32).astype(jnp.bfloat16)
    packed = jnp.dot(placer, tokens[...], preferred_element_type=jnp.float32).astype(jnp.bfloat16)
    straight[...] = packed[: slots // 2]
    crossed[...] = packed[slots // 2 :]


def pack(tokens, route, capacity):
    count, width = tokens.shape
    slots = lax.axis_size("expert") * capacity
    in_vmem = pl.BlockSpec(memory_space=pltpu.VMEM)
    half = jax.ShapeDtypeStruct((slots // 2, width), tokens.dtype)
    straight, crossed, slot_of = pl.pallas_call(
        functools.partial(pack_kernel, capacity),
        out_shape=[half, half, jax.ShapeDtypeStruct((1, count), jnp.int32)],
        in_specs=[in_vmem] * 2,
        out_specs=[in_vmem] * 3,
        cost_estimate=pl.CostEstimate(
            flops=PACK_FLOPS, bytes_accessed=4 * tokens.size, transcendentals=0
        ),
        compiler_params=pltpu.CompilerParams(vmem_limit_bytes=VMEM_LIMIT),
        name="pack",
    )(tokens, (route[:, 0] ^ lax.axis_index("expert")).reshape(1, count))
    return straight, crossed, slot_of.reshape(count)


def fold_kernel(capacity, straight, crossed, *outs):
    for j, out in enumerate(outs):
        rows = pl.ds(j * capacity, capacity)
        out[:capacity] = straight[rows]
        out[capacity:] = crossed[rows]


def fold(straight, crossed, capacity):
    in_vmem = pl.BlockSpec(memory_space=pltpu.VMEM)
    out = jax.ShapeDtypeStruct((2 * capacity, straight.shape[1]), straight.dtype)
    return pl.pallas_call(
        functools.partial(fold_kernel, capacity),
        out_shape=[out] * (straight.shape[0] // capacity),
        in_specs=[in_vmem] * 2,
        out_specs=[in_vmem] * (straight.shape[0] // capacity),
        cost_estimate=pl.CostEstimate(
            flops=FOLD_FLOPS, bytes_accessed=8 * straight.size, transcendentals=0
        ),
        compiler_params=pltpu.CompilerParams(vmem_limit_bytes=VMEM_LIMIT),
        name="fold",
    )(straight, crossed)


def pipelined_shards(tokens, route, route_weight, gate_up, down):
    n_expert = lax.axis_size("expert")
    tok_rows = tokens.shape[0]
    capacity = max(2, 3 * tok_rows // (2 * n_expert))
    slots = n_expert * capacity
    straight, crossed, slot_of = pack(tokens, route, capacity)
    crossed = flip(crossed, "expert", 1)

    folded = fold(straight, crossed, capacity)
    received = [r if j == 0 else flip(r, "expert", 2 * j) for j, r in enumerate(folded)]

    count = 2 * capacity
    subs = [gather(received[s], FORMS[s][0]) for s in range(SUBS)]
    weights = (gate_up, down)
    results = [None] * SUBS
    for group in GROUPS:
        chunks = [(count, subs[s], *sent_first(FORMS[s][1], count)) for s in group]
        partials = expert_layer(weights, chunks)
        for s, arrays in zip(group, partials):
            terms = sums(FORMS[s][1], arrays)
            total = terms[0]
            for term in terms[1:]:
                total = total + term.astype(jnp.float32)
            results[s] = total.astype(jnp.bfloat16)

    straight, crossed = [], []
    for s in range(SUBS):
        mine, other = results[s][:capacity], results[s][capacity:]
        if s == 0:
            other = flip(other, "expert", 1)
        else:
            mine = flip(mine, "expert", 2 * s)
            other = flip(other, "expert", 2 * s + 1)
        straight.append(mine)
        crossed.append(other)
    returned = straight + crossed
    picker = (slot_of[:, None] == jnp.arange(slots, dtype=jnp.int32)[None, :]).astype(jnp.bfloat16)
    gathered = jnp.dot(picker, jnp.concatenate(returned), preferred_element_type=jnp.float32)
    return (route_weight[:, None] * gathered).astype(jnp.bfloat16)


def solution(mesh):
    in_specs = (
        P("expert", "pipe"),
        P("expert", None),
        P("expert"),
        P("expert", None, "pipe", None),
        P("expert", "pipe", None),
    )
    out_specs = P("expert", "pipe")

    def shards(tokens, route, route_weight, gate_up, down):
        n_expert, n_pipe = mesh.shape["expert"], mesh.shape["pipe"]
        tok_rows, width = tokens.shape
        capacity = max(2, 3 * tok_rows // (2 * n_expert))
        powers = n_expert & (n_expert - 1) == 0 and n_pipe & (n_pipe - 1) == 0
        aligned = width % 128 == 0 and capacity % 8 == 0 and gate_up.shape[2] % 128 == 0
        if powers and aligned and n_expert == 2 * SUBS and n_pipe == 4:
            return pipelined_shards(tokens, route, route_weight, gate_up, down)
        return serial_shards(tokens, route, route_weight, gate_up, down)

    return jax.shard_map(shards, mesh=mesh, in_specs=in_specs, out_specs=out_specs, check_vma=False)
```

```python
import functools

import jax
import jax.numpy as jnp
from jax import lax
from jax.experimental import pallas as pl
from jax.experimental.pallas import tpu as pltpu
from jax.sharding import PartitionSpec as P


SUBS = 4
VMEM_LIMIT = 32 << 20
PACK_FLOPS = 1 << 33
FORMS = (('3', '2'), ('2', '2'), ('3', '3'), ('3', '3'))
GROUPS = ((3,), (2,), (1, 0))


def serial_shards(tokens, route, route_weight, gate_up, down):
    n_expert = lax.axis_size("expert")
    tok_rows = tokens.shape[0]
    width_part = tokens.shape[1]
    capacity = max(2, 3 * tok_rows // (2 * n_expert))
    slot_total = n_expert * capacity
    chosen = route[:, 0]
    onehot = (chosen[:, None] == jnp.arange(n_expert, dtype=jnp.int32)[None, :]).astype(jnp.int32)
    position = jnp.sum(jnp.cumsum(onehot, axis=0) * onehot, axis=1) - 1
    slot_of = chosen * capacity + position
    placer = (slot_of[None, :] == jnp.arange(slot_total, dtype=jnp.int32)[:, None]).astype(
        jnp.bfloat16
    )
    packed = jnp.dot(placer, tokens, preferred_element_type=jnp.float32).astype(jnp.bfloat16)
    packed = packed.reshape(n_expert, capacity, width_part)
    local_in = gate_up[0]
    local_out = down[0]
    received = lax.all_to_all(packed, "expert", split_axis=0, concat_axis=0, tiled=True)
    sources, items, cols = received.shape
    flat_rows = received.reshape(sources * items, cols)
    both = jnp.einsum(
        "rd,sfd->rsf",
        lax.all_gather(flat_rows, "pipe", axis=1, tiled=True),
        local_in,
        preferred_element_type=jnp.float32,
    )
    hidden = (jax.nn.silu(both[:, 0]) * both[:, 1]).astype(jnp.bfloat16)
    partial_value = jnp.dot(hidden, local_out, preferred_element_type=jnp.float32)
    result = lax.psum_scatter(partial_value, "pipe", scatter_dimension=1, tiled=True).astype(
        jnp.bfloat16
    )
    result = result.reshape(sources, items, cols)
    returned = lax.all_to_all(result, "expert", split_axis=0, concat_axis=0, tiled=True)
    gathered = jnp.dot(
        placer.T, returned.reshape(slot_total, width_part), preferred_element_type=jnp.float32
    )
    return (route_weight[:, None] * gathered).astype(jnp.bfloat16)


def flip(x, axis, mask):
    return lax.ppermute(x, axis, [(i, i ^ mask) for i in range(lax.axis_size(axis))])


def expert_kernel(plan, n_pipe, *refs):
    gate_up, down = refs[:2]
    me = lax.axis_index("pipe")
    width = down.shape[2] // n_pipe

    core = lax.axis_index("expert") & 1
    idents = [0, 1 + core, 2 - core, 3]

    def columns(piece):
        return pl.ds(pl.multiple_of((me ^ idents[piece]) * width, 128), width)

    gate = up = None
    for piece in range(n_pipe):
        rows = [refs[i][r : r + n] for _, parts, _ in plan for i, r, n in parts[piece]]
        rows = jnp.concatenate(rows) if len(rows) > 1 else rows[0]
        products = []
        for s in range(2):
            products.append(
                lax.dot_general(
                    rows,
                    gate_up[0, s, :, columns(piece)],
                    (((1,), (1,)), ((), ())),
                    preferred_element_type=jnp.float32,
                )
            )
        gate = products[0] if piece == 0 else gate + products[0]
        up = products[1] if piece == 0 else up + products[1]
    hidden = (gate / (1.0 + jnp.exp(-gate)) * up).astype(jnp.bfloat16)
    for piece in range(n_pipe):
        product = jnp.dot(hidden, down[0, :, columns(piece)], preferred_element_type=jnp.float32)
        first = 0
        for _, _, results in plan:
            for i, r, n in results[piece]:
                refs[i][r : r + n] = product[first : first + n].astype(refs[i].dtype)
                first += n


def expert_layer(weights, chunks):
    n_pipe = lax.axis_size("pipe")
    width = weights[1].shape[2] // n_pipe
    operands, shapes, plan = list(weights), [], []
    for _, parts, _, _ in chunks:
        for segments in parts:
            for array, _, _ in segments:
                if all(array is not o for o in operands):
                    operands.append(array)

    def place(array):
        return [array is o for o in operands].index(True)

    for count, parts, sent, kept in chunks:
        results = [[] for _ in range(n_pipe)]
        for blocks in [*sent, *[[(i, count)] for i in kept]]:
            at = 0
            for ident, rows in blocks:
                results[ident].append((len(operands) + len(shapes), at, rows))
                at += rows
            kind = jnp.bfloat16 if blocks in sent else jnp.float32
            shapes.append(jax.ShapeDtypeStruct((at, width), kind))
        plan.append((count, [[(place(a), r, n) for a, r, n in p] for p in parts], results))
    total = sum(p[0] for p in plan)
    size = sum(w.size for w in weights)
    in_vmem = pl.BlockSpec(memory_space=pltpu.VMEM)
    outs = pl.pallas_call(
        functools.partial(expert_kernel, plan, n_pipe),
        out_shape=shapes,
        in_specs=[in_vmem] * len(operands),
        out_specs=[in_vmem] * len(shapes),
        cost_estimate=pl.CostEstimate(
            flops=2 * total * size, bytes_accessed=2 * size, transcendentals=0
        ),
        compiler_params=pltpu.CompilerParams(vmem_limit_bytes=VMEM_LIMIT),
        name="expert_layer",
    )(*operands)
    outs = list(outs)
    return [[outs.pop(0) for _ in [*sent, *kept]] for _, _, sent, kept in chunks]


def swap(x, stage):
    n_pipe, n_expert = lax.axis_size("pipe"), lax.axis_size("expert")
    pairs = []
    for p in range(n_pipe):
        for e in range(n_expert):
            bit = 1 + (e & 1 ^ stage)
            pairs.append((p * n_expert + e, (p ^ bit) * n_expert + e))
    return lax.ppermute(x, ("pipe", "expert"), pairs)


def gather(own, form):
    count = own.shape[0]
    moved = swap(own, 0)
    if form == "3":
        straight = swap(own, 1)
        across = swap(moved, 1)
        return [[(a, 0, count)] for a in (own, moved, straight, across)]
    pair = jnp.concatenate([own, moved])
    pair = swap(pair, 1)
    return [[(own, 0, count)], [(moved, 0, count)], [(pair, 0, count)], [(pair, count, count)]]


def sent_first(form, count):
    if form == "3":
        return [[(3, count)], [(1, count)]], [2, 0]
    return [[(1, count), (3, count)]], [2, 0]


def sums(form, arrays):
    wide, narrow = jnp.float32, jnp.bfloat16
    *sent, piece, own = arrays
    count = own.shape[0]
    if form == "3":
        far = swap(sent[0], 0)
        near = swap(sent[1], 0)
        piece = (piece + far.astype(wide)).astype(narrow)
        return own, near, swap(piece, 1)
    pair = swap(sent[0], 0)
    piece = (piece + pair[count:].astype(wide)).astype(narrow)
    return own, pair[:count], swap(piece, 1)


def pack_kernel(capacity, tokens, distance, *outs):
    *blocks, slot_of = outs
    count = tokens.shape[0]
    n_expert = len(blocks)
    slots = n_expert * capacity
    distance = distance[...]
    experts = lax.broadcasted_iota(jnp.int32, (n_expert, count), 0)
    onehot = (experts == distance).astype(jnp.float32)
    before = lax.broadcasted_iota(jnp.int32, (count, count), 0)
    after = lax.broadcasted_iota(jnp.int32, (count, count), 1)
    upto = (before <= after).astype(jnp.float32).astype(jnp.bfloat16)
    ranks = jnp.dot(onehot.astype(jnp.bfloat16), upto, preferred_element_type=jnp.float32)
    position = jnp.sum(ranks * onehot, axis=0, keepdims=True).astype(jnp.int32) - 1
    slot = distance * capacity + position
    slot_of[...] = slot
    rows = lax.broadcasted_iota(jnp.int32, (slots, count), 0)
    placer = (rows == slot).astype(jnp.float32).astype(jnp.bfloat16)
    packed = jnp.dot(placer, tokens[...], preferred_element_type=jnp.float32).astype(jnp.bfloat16)
    for k, block in enumerate(blocks):
        block[...] = packed[k * capacity : (k + 1) * capacity]


def pack(tokens, route, capacity):
    count, width = tokens.shape
    n_expert = lax.axis_size("expert")
    in_vmem = pl.BlockSpec(memory_space=pltpu.VMEM)
    block = jax.ShapeDtypeStruct((capacity, width), tokens.dtype)
    *blocks, slot_of = pl.pallas_call(
        functools.partial(pack_kernel, capacity),
        out_shape=[block] * n_expert + [jax.ShapeDtypeStruct((1, count), jnp.int32)],
        in_specs=[in_vmem] * 2,
        out_specs=[in_vmem] * (n_expert + 1),
        cost_estimate=pl.CostEstimate(
            flops=PACK_FLOPS, bytes_accessed=4 * tokens.size, transcendentals=0
        ),
        compiler_params=pltpu.CompilerParams(vmem_limit_bytes=VMEM_LIMIT),
        name="pack",
    )(tokens, (route[:, 0] ^ lax.axis_index("expert")).reshape(1, count))
    return blocks, slot_of.reshape(count)


def join_kernel(first, second, out):
    count = first.shape[0]
    out[:count] = first[...]
    out[count:] = second[...]


def join(first, second):
    in_vmem = pl.BlockSpec(memory_space=pltpu.VMEM)
    return pl.pallas_call(
        join_kernel,
        out_shape=jax.ShapeDtypeStruct((2 * first.shape[0], first.shape[1]), first.dtype),
        in_specs=[in_vmem] * 2,
        out_specs=in_vmem,
        cost_estimate=pl.CostEstimate(
            flops=0, bytes_accessed=8 * first.size, transcendentals=0
        ),
        compiler_params=pltpu.CompilerParams(vmem_limit_bytes=VMEM_LIMIT),
        name="join",
    )(first, second)


def pipelined_shards(tokens, route, route_weight, gate_up, down):
    n_expert = lax.axis_size("expert")
    tok_rows = tokens.shape[0]
    capacity = max(2, 3 * tok_rows // (2 * n_expert))
    slots = n_expert * capacity
    blocks, slot_of = pack(tokens, route, capacity)
    blocks = [b if k == 0 else flip(b, "expert", k) for k, b in enumerate(blocks)]
    received = []
    for j in range(SUBS):
        received.append(join(blocks[2 * j], blocks[2 * j + 1]))

    count = 2 * capacity
    subs = [gather(received[s], FORMS[s][0]) for s in range(SUBS)]
    weights = (gate_up, down)
    results = [None] * SUBS
    for group in GROUPS:
        chunks = [(count, subs[s], *sent_first(FORMS[s][1], count)) for s in group]
        partials = expert_layer(weights, chunks)
        for s, arrays in zip(group, partials):
            terms = sums(FORMS[s][1], arrays)
            total = terms[0]
            for term in terms[1:]:
                total = total + term.astype(jnp.float32)
            results[s] = total.astype(jnp.bfloat16)

    returned = []
    for s in range(SUBS):
        mine, other = results[s][:capacity], results[s][capacity:]
        if s == 0:
            other = flip(other, "expert", 1)
        else:
            mine = flip(mine, "expert", 2 * s)
            other = flip(other, "expert", 2 * s + 1)
        returned += [mine, other]
    picker = (slot_of[:, None] == jnp.arange(slots, dtype=jnp.int32)[None, :]).astype(jnp.bfloat16)
    gathered = jnp.dot(picker, jnp.concatenate(returned), preferred_element_type=jnp.float32)
    return (route_weight[:, None] * gathered).astype(jnp.bfloat16)


def solution(mesh):
    in_specs = (
        P("expert", "pipe"),
        P("expert", None),
        P("expert"),
        P("expert", None, "pipe", None),
        P("expert", "pipe", None),
    )
    out_specs = P("expert", "pipe")

    def shards(tokens, route, route_weight, gate_up, down):
        n_expert, n_pipe = mesh.shape["expert"], mesh.shape["pipe"]
        tok_rows, width = tokens.shape
        capacity = max(2, 3 * tok_rows // (2 * n_expert))
        powers = n_expert & (n_expert - 1) == 0 and n_pipe & (n_pipe - 1) == 0
        aligned = width % 128 == 0 and capacity % 8 == 0 and gate_up.shape[2] % 128 == 0
        if powers and aligned and n_expert == 2 * SUBS and n_pipe == 4:
            return pipelined_shards(tokens, route, route_weight, gate_up, down)
        return serial_shards(tokens, route, route_weight, gate_up, down)

    return jax.shard_map(shards, mesh=mesh, in_specs=in_specs, out_specs=out_specs, check_vma=False)
```
